32 devices in a mesh: dp: 4 (over z), expert: 8 (over y, x, core).
Axes of the slice: x: 2, y: 2, z: 4, core: 2. Of those that a mesh axis runs over, the one named last changes fastest.
Arguments:
- out_grad: bfloat16 [8192, 4096], P(('dp', 'expert')), may hold values from -6 to 6
- destination: int32 [8192, 1], P(('dp', 'expert')), may hold values from 0 to 7; in each aligned block of 256 rows (0 to 255, 256 to 511, ...) at most 64 rows name the same one
- hidden: bfloat16 [16384, 1024], P(('dp', 'expert')), may hold values from -6 to 6
- weight: bfloat16 [8, 1024, 4096], P('expert', None, 'dp'), may hold values from -0.09375 to 0.09375
- left_prev: float32 [8, 2048, 1024], P('expert', 'dp'), may hold values from -3 to 3
- right_prev: float32 [8, 4096, 2048], P('expert', 'dp'), may hold values from -3 to 3
Outputs:
- grad_rows: bfloat16 [8192, 1024], P(('dp', 'expert'))
- left_stats: float32 [8, 2048, 1024], P('expert', 'dp')
- right_stats: float32 [8, 4096, 2048], P('expert', 'dp')
The draws below stay inside these ranges and needn't reach their ends.
Inputs may be any that keep to these rules, and one draw needn't show every extreme that they name: Among the rows of one device at most 64 have the same destination, and on some device that many do.
All inputs are finite; a program needn't handle non-finite values.
Results may differ from the reference program's by a relative error of at most 0.001.
Values may be sent and summed in bfloat16 or wider, within the bound.
A program may use at most 128 MiB of HBM per device.

```python
import math
import jax
import jax.numpy as jnp
import numpy as np
from jax import lax

D = 4096
F = 1024
ROWS = 256
EXPERTS = 8
CAP = 64
RECV = 512
BLOCK = 2048
NBLK = 2
N_DP = 4


def steps_of(key, dims, split, smallest, top_value):
    def one(axis_at, parts):
        draws = jax.random.uniform(jax.random.fold_in(jax.random.fold_in(key, 6), axis_at), (parts,), jnp.float32, smallest / len(split), top_value / len(split))
        return jnp.repeat(jnp.exp(draws), dims[axis_at] // parts).reshape((-1,) + (1,) * (len(dims) - axis_at - 1))

    level = one(*split[0])
    for cut in split[1:]:
        level = level * one(*cut)
    return level


def shared_out(key, own, number, rows, number_of, top, most, skew):
    ranking = jax.random.permutation(key, number_of)
    packed, usual = shares(number_of, rows * top, most, skew, True), shares(number_of, rows * top, most, skew, False)
    places = jnp.arange(number_of)

    def named(tallies, turn):
        used = int((tallies > 0).sum())
        fixed = max(1, used // 4)
        passed = fixed + (places - fixed + turn * (used - fixed)) % max(1, number_of - fixed)
        return jnp.zeros((number_of,), jnp.int32).at[ranking[jnp.where(places < fixed, places, passed)]].set(jnp.asarray(tallies, jnp.int32))

    tallies = jnp.where(number % 4 == 0, named(packed, number // 4), named(usual, number - number // 4 - 1))
    mixed = jax.random.permutation(jax.random.fold_in(own, 3), number_of)
    source_of, taker = mixed[0:number_of // 2 * 2:2], mixed[1:number_of // 2 * 2:2]
    slack = jnp.minimum(tallies[source_of] - 1, most - tallies[taker]) // 2
    slack = jnp.where((source_of == ranking[0]) | (taker == ranking[0]) | (tallies[taker] == 0), 0, jnp.maximum(slack, 0))
    passed = jax.random.randint(jax.random.fold_in(own, 4), (number_of // 2,), 0, 1 << 20) % (slack + 1)
    tallies = tallies.at[source_of].add(-passed).at[taker].add(passed)
    members = jnp.searchsorted(jnp.cumsum(tallies), jnp.arange(rows * top), side="right").astype(jnp.int32)
    table = members.reshape(top, rows).T
    table = table[jax.random.permutation(jax.random.fold_in(own, 1), rows)]
    turn = jax.random.randint(jax.random.fold_in(own, 2), (rows, 1), 0, top)
    return jnp.take_along_axis(table, (jnp.arange(top)[None, :] + turn) % top, axis=1)


def shares(amount, total, limit, slope, full):
    weights = [(1 << 20) // math.isqrt(rank ** slope) + 1 for rank in range(1, amount + 1)]
    largest = limit if full else min(limit, max(-(-total // amount), total * weights[0] // sum(weights)))
    least = 1 if total - largest >= amount - 1 else 0
    holding, rest = [largest] + [least] * (amount - 1), total - largest - least * (amount - 1)
    while rest > 0:
        free = [i for i in range(1, amount) if holding[i] < largest] or [i for i in range(1, amount) if holding[i] < limit]
        mass, left = sum([weights[i] for i in free]), rest
        for i in free:
            extra = min(limit - holding[i], max(1, left * weights[i] // mass), rest)
            holding[i] = holding[i] + extra
            rest = rest - extra
    return np.array(holding)


def noise(rng, shape, deviation, most, shards=(), held_as=jnp.bfloat16):
    array = jax.random.normal(rng, shape, jnp.float32) * deviation
    if len(shards) > 0:
        array = steps_of(rng, shape, shards, -0.22, 0.18) * array
    return jnp.clip(array, min=-most, max=most).astype(held_as)


def setup_inputs(seed: int = 0) -> dict:
    keys = jax.random.split(jax.random.key(seed), 7)
    out_grad = noise(keys[0], (N_DP * EXPERTS * ROWS, D), 1.0, 6.0, ((0, 32),))
    destination_keys = jax.random.split(jax.random.fold_in(keys[1], 1), (N_DP * EXPERTS * ROWS) // ROWS)
    destination_turns = jax.random.permutation(jax.random.fold_in(keys[1], 3), (N_DP * EXPERTS * ROWS) // ROWS)
    destination = jax.vmap(lambda own, number: shared_out(jax.random.fold_in(keys[1], 2), own, number, ROWS, EXPERTS, 1, CAP, 2))(destination_keys, destination_turns).reshape((N_DP * EXPERTS * ROWS, 1))
    hidden = noise(keys[2], (N_DP * EXPERTS * RECV, F), 1.0, 6.0, ((0, 32),))
    weight = noise(keys[3], (EXPERTS, F, D), D ** -0.5, 0.09375, ((0, 8), (2, 4)))
    left_prev = noise(keys[4], (EXPERTS, NBLK * F, F), 0.2, 3.0, ((0, 8), (1, 4)), jnp.float32)
    right_prev = noise(keys[5], (EXPERTS, NBLK * BLOCK, BLOCK), 0.2, 3.0, ((0, 8), (1, 4)), jnp.float32)
    return {"out_grad": out_grad, "destination": destination, "hidden": hidden, "weight": weight, "left_prev": left_prev, "right_prev": right_prev}


ema_decay = 0.9


def reference(out_grad, destination, hidden, weight, left_prev, right_prev):
    group_rows = out_grad.reshape(N_DP, EXPERTS * ROWS, D)
    dest_all = destination.reshape(N_DP, EXPERTS, ROWS)
    expert_ids = jnp.arange(EXPERTS, dtype=jnp.int32)
    choose = (dest_all[..., None] == expert_ids).astype(jnp.int32)
    before = jnp.cumsum(choose, axis=2) - choose
    slot_rank = jnp.sum(before * choose, axis=3)
    source_ids = jnp.arange(EXPERTS, dtype=jnp.int32)[None, :, None]
    slot_index = (source_ids * CAP + slot_rank).reshape(N_DP, EXPERTS * ROWS).astype(jnp.int32)
    dest_flat = dest_all.reshape(N_DP, EXPERTS * ROWS).astype(jnp.int32)
    hidden_all = hidden.reshape(N_DP, EXPERTS, RECV, F).transpose(1, 0, 2, 3)
    scale_left = 1.0 / (N_DP * ROWS * BLOCK)
    scale_right = 1.0 / (N_DP * ROWS * F)

    def place(rows_in, target_row):
        return jnp.zeros((RECV, D), jnp.bfloat16).at[target_row].set(rows_in, mode="drop")

    def one_expert(operands):
        expert_id, expert_weight, expert_hidden, left_old, right_old = operands
        target = jnp.where(dest_flat == expert_id, slot_index, RECV).astype(jnp.int32)
        arrived = jax.vmap(place)(group_rows, target)
        arrived_wide = arrived.astype(jnp.float32)
        slot_grad = jnp.einsum("grd,fd->grf", arrived_wide, expert_weight.astype(jnp.float32)).astype(jnp.bfloat16)
        weight_grad = jnp.einsum("grf,grd->fd", expert_hidden.astype(jnp.float32), arrived_wide)
        grad_blocks = weight_grad.reshape(F, NBLK, BLOCK).transpose(1, 0, 2)
        left_gram = jnp.einsum("bfc,bgc->bfg", grad_blocks, grad_blocks, precision=lax.Precision.HIGHEST) * scale_left
        right_gram = jnp.einsum("bfc,bfd->bcd", grad_blocks, grad_blocks, precision=lax.Precision.HIGHEST) * scale_right
        left_slots = left_gram.reshape(NBLK * F, F)
        right_slots = right_gram.reshape(NBLK * BLOCK, BLOCK)
        left_new = ema_decay * left_old + (1.0 - ema_decay) * left_slots
        right_new = ema_decay * right_old + (1.0 - ema_decay) * right_slots
        return slot_grad, left_new, right_new

    slot_grads, left_stats, right_stats = lax.map(one_expert, (expert_ids, weight, hidden_all, left_prev, right_prev))
    group_ids = jnp.arange(N_DP, dtype=jnp.int32)[:, None]
    grad_rows = slot_grads[dest_flat, group_ids, slot_index]
    return grad_rows.reshape(N_DP * EXPERTS * ROWS, F), left_stats, right_stats
```

```python
import functools

import jax
import jax.numpy as jnp
from jax import lax
from jax.experimental import pallas as pl
from jax.experimental.pallas import tpu as pltpu
from jax.sharding import PartitionSpec as P

MESH = pl.DeviceIdType.MESH
ema_decay = 0.9


def swapped(value, axis, distance):
    mask = 2**distance
    pairs = [(source, source ^ mask) for source in range(lax.axis_size(axis))]
    return lax.ppermute(value, axis, pairs)


def slot_choice(dest, expert_count, capacity):
    row_count = dest.shape[-1]
    choose = dest[..., None] == jnp.arange(expert_count, dtype=jnp.int32)
    earlier = jnp.tril(jnp.ones((row_count, row_count), jnp.bfloat16), -1)
    before = jnp.einsum(
        "rq,...qe->...re", earlier, choose.astype(jnp.bfloat16), preferred_element_type=jnp.float32
    )
    rank = jnp.sum(jnp.where(choose, before, 0.0), axis=-1).astype(jnp.int32)
    slots = dest * capacity + rank
    ids = jnp.arange(expert_count * capacity, dtype=jnp.int32)
    return slots, (ids[:, None] == slots[..., None, :]).astype(jnp.bfloat16)


def greet(peers):
    barrier = pltpu.get_barrier_semaphore()
    for peer in peers:
        pl.semaphore_signal(barrier, inc=1, device_id=peer, device_id_type=MESH)
    pl.semaphore_wait(barrier, len(peers))


def send(source, target, sends, receives, at, peer):
    copy = pltpu.make_async_remote_copy(
        src_ref=source,
        dst_ref=target,
        send_sem=sends.at[at],
        recv_sem=receives.at[at],
        device_id=peer,
        device_id_type=MESH,
    )
    copy.start()
    return copy


def first_kernel(
    groups, experts, rows, dest, slots, columns, dest_all, arrived, sends, receives, own
):
    g, e = lax.axis_index("dp"), lax.axis_index("expert")
    width = rows.shape[1] // groups
    others = [lax.rem(g + k, groups) for k in range(1, groups)]
    mates = [lax.rem(e + k, experts) for k in range(1, experts)]
    greet([{"dp": o} for o in others] + [{"expert": m} for m in mates])
    copies = []
    for o in others:
        copies.append(send(dest, dest_all.at[g], sends, receives, len(copies), {"dp": o}))
    for o in others:
        part = rows.at[:, pl.ds(pl.multiple_of(o * width, width), width)]
        copies.append(send(part, columns.at[g], sends, receives, len(copies), {"dp": o}))
    for m in mates:
        copies.append(send(slots.at[m], arrived.at[e], sends, receives, len(copies), {"expert": m}))
    mine = rows.at[:, pl.ds(pl.multiple_of(g * width, width), width)]
    local_copies = [
        pltpu.make_async_copy(dest, dest_all.at[g], own.at[0]),
        pltpu.make_async_copy(mine, columns.at[g], own.at[1]),
        pltpu.make_async_copy(slots.at[e], arrived.at[e], own.at[2]),
    ]
    for copy in local_copies:
        copy.start()
    for copy in copies:
        copy.wait()
    for copy in local_copies:
        copy.wait()


def first_exchange(rows, dest, slots, groups, experts):
    row_count, model_width = rows.shape
    count = 2 * (groups - 1) + experts - 1
    anywhere = pl.BlockSpec(memory_space=pl.ANY)
    return pl.pallas_call(
        functools.partial(first_kernel, groups, experts),
        out_shape=(
            jax.ShapeDtypeStruct((groups, row_count, model_width // groups), rows.dtype),
            jax.ShapeDtypeStruct((groups,) + dest.shape, dest.dtype),
            jax.ShapeDtypeStruct(slots.shape, slots.dtype),
        ),
        in_specs=[anywhere] * 3,
        out_specs=(anywhere,) * 3,
        scratch_shapes=[
            pltpu.SemaphoreType.DMA((count,)),
            pltpu.SemaphoreType.DMA((count,)),
            pltpu.SemaphoreType.DMA((3,)),
        ],
        compiler_params=pltpu.CompilerParams(collective_id=1, has_side_effects=True),
        name="first_exchange",
    )(rows, dest, slots)


def second_kernel(experts, slots, arrived, sends, receives, own):
    e = lax.axis_index("expert")
    mates = [lax.rem(e + k, experts) for k in range(1, experts)]
    greet([{"expert": m} for m in mates])
    copies = []
    for m in mates:
        copies.append(
            send(slots.at[:, m], arrived.at[:, e], sends, receives, len(copies), {"expert": m})
        )
    local_copy = pltpu.make_async_copy(slots.at[:, e], arrived.at[:, e], own)
    local_copy.start()
    for copy in copies:
        copy.wait()
    local_copy.wait()


def second_exchange(slots, experts):
    anywhere = pl.BlockSpec(memory_space=pl.ANY)
    return pl.pallas_call(
        functools.partial(second_kernel, experts),
        out_shape=jax.ShapeDtypeStruct(slots.shape, slots.dtype),
        in_specs=[anywhere],
        out_specs=anywhere,
        scratch_shapes=[
            pltpu.SemaphoreType.DMA((experts - 1,)),
            pltpu.SemaphoreType.DMA((experts - 1,)),
            pltpu.SemaphoreType.DMA,
        ],
        compiler_params=pltpu.CompilerParams(collective_id=2, has_side_effects=True),
        name="second_exchange",
    )(slots)


def local(out_grad, destination, hidden, weight, left_prev, right_prev):
    expert_count = lax.axis_size("expert")
    group_count = lax.axis_size("dp")
    row_count, model_width = out_grad.shape
    slot_count, hidden_width = hidden.shape
    capacity = slot_count // expert_count
    half_width = model_width // group_count
    block_width = 2 * half_width

    hidden_all = lax.all_gather(hidden, "dp", axis=0, tiled=True)
    target_slots, own_choice = slot_choice(destination[:, 0], expert_count, capacity)
    outgoing = jnp.dot(own_choice, out_grad, preferred_element_type=jnp.float32).astype(
        out_grad.dtype
    )
    column_rows, dest_all, arrived = first_exchange(
        out_grad,
        destination.reshape(row_count // 128, 128),
        outgoing.reshape(expert_count, capacity, model_width),
        group_count,
        expert_count,
    )
    arrived = arrived.reshape(slot_count, model_width)
    weight_late, column_rows = lax.optimization_barrier((weight[0], column_rows))
    weight_all = lax.all_gather(weight_late, "dp", axis=0)

    _, all_choice = slot_choice(dest_all.reshape(group_count, row_count), expert_count, capacity)
    column_slots = lax.dot_general(
        all_choice,
        column_rows,
        (((2,), (1,)), ((0,), (0,))),
        preferred_element_type=jnp.float32,
    ).astype(out_grad.dtype)
    columns = second_exchange(
        column_slots.reshape(group_count, expert_count, capacity, half_width), expert_count
    )
    hidden_slots = hidden_all
    own_piece = lax.dot_general(
        columns.reshape(-1, half_width),
        hidden_slots,
        (((0,), (0,)), ((), ())),
        preferred_element_type=jnp.float32,
    ).astype(jnp.bfloat16)
    partner = swapped(own_piece, "dp", 0)
    parity = lax.axis_index("dp") % 2
    upper_half = parity == 0
    first_half = jnp.where(upper_half, own_piece, partner)
    second_half = jnp.where(upper_half, partner, own_piece)
    block_grad = jnp.concatenate([first_half, second_half], axis=0)
    scale_left = 1.0 / (group_count * row_count * block_width)
    scale_right = 1.0 / (group_count * row_count * hidden_width)
    right_gram = (
        lax.dot_general(
            own_piece,
            block_grad,
            (((1,), (1,)), ((), ())),
            preferred_element_type=jnp.float32,
        )
        * scale_right
    )
    half_hidden = hidden_width // 2
    hidden_cols = lax.dynamic_slice_in_dim(block_grad, parity * half_hidden, half_hidden, 1)
    left_gram = (
        lax.dot_general(
            hidden_cols,
            block_grad,
            (((0,), (0,)), ((), ())),
            preferred_element_type=jnp.float32,
        )
        * scale_left
    )
    left_stats = ema_decay * left_prev + (1.0 - ema_decay) * left_gram[None]
    right_stats = ema_decay * right_prev + (1.0 - ema_decay) * right_gram[None]

    arrived, _, _ = lax.optimization_barrier((arrived, left_stats, right_stats))
    slot_grad = sum(
        lax.dot_general(
            arrived[:, part * half_width : (part + 1) * half_width],
            weight_all[part],
            (((1,), (1,)), ((), ())),
            preferred_element_type=jnp.float32,
        )
        for part in range(group_count)
    ).astype(jnp.bfloat16)
    returned = lax.all_to_all(
        slot_grad.reshape(expert_count, capacity, hidden_width),
        "expert",
        split_axis=0,
        concat_axis=0,
        tiled=True,
    )
    grad_rows = returned.reshape(slot_count, hidden_width)[target_slots]
    return (grad_rows, left_stats, right_stats)


def solution(mesh):
    placed = (
        P(("dp", "expert"), None),
        P(("dp", "expert"), None),
        P(("dp", "expert"), None),
        P("expert", None, "dp"),
        P("expert", "dp", None),
        P("expert", "dp", None),
    )
    return jax.shard_map(
        local,
        mesh=mesh,
        in_specs=placed,
        out_specs=(P(("dp", "expert"), None), P("expert", "dp", None), P("expert", "dp", None)),
        check_vma=False,
    )
```

```python
import functools

import jax
import jax.numpy as jnp
from jax import lax
from jax.experimental import pallas as pl
from jax.experimental.pallas import tpu as pltpu
from jax.sharding import PartitionSpec as P

MESH = pl.DeviceIdType.MESH
ema_decay = 0.9


def swapped(value, axis, distance):
    mask = 2**distance
    pairs = [(source, source ^ mask) for source in range(lax.axis_size(axis))]
    return lax.ppermute(value, axis, pairs)


def slot_choice(dest, expert_count, capacity):
    row_count = dest.shape[-1]
    choose = dest[..., None] == jnp.arange(expert_count, dtype=jnp.int32)
    earlier = jnp.tril(jnp.ones((row_count, row_count), jnp.bfloat16), -1)
    before = jnp.einsum(
        "rq,...qe->...re", earlier, choose.astype(jnp.bfloat16), preferred_element_type=jnp.float32
    )
    rank = jnp.sum(jnp.where(choose, before, 0.0), axis=-1).astype(jnp.int32)
    slots = dest * capacity + rank
    ids = jnp.arange(expert_count * capacity, dtype=jnp.int32)
    return slots, (ids[:, None] == slots[..., None, :]).astype(jnp.bfloat16)


def greet(peers):
    barrier = pltpu.get_barrier_semaphore()
    for peer in peers:
        pl.semaphore_signal(barrier, inc=1, device_id=peer, device_id_type=MESH)
    pl.semaphore_wait(barrier, len(peers))


def send(source, target, sends, receives, at, peer):
    copy = pltpu.make_async_remote_copy(
        src_ref=source,
        dst_ref=target,
        send_sem=sends.at[at],
        recv_sem=receives.at[at],
        device_id=peer,
        device_id_type=MESH,
    )
    copy.start()
    return copy


def first_kernel(
    groups, experts, rows, dest, slots, columns, dest_all, arrived, sends, receives, own
):
    g, e = lax.axis_index("dp"), lax.axis_index("expert")
    width = rows.shape[1] // groups
    others = [lax.rem(g + k, groups) for k in range(1, groups)]
    mates = [lax.rem(e + k, experts) for k in range(1, experts)]
    greet([{"dp": o} for o in others] + [{"expert": m} for m in mates])
    copies = []
    for o in others:
        copies.append(send(dest, dest_all.at[g], sends, receives, len(copies), {"dp": o}))
    for o in others:
        part = rows.at[:, pl.ds(pl.multiple_of(o * width, width), width)]
        copies.append(send(part, columns.at[g], sends, receives, len(copies), {"dp": o}))
    for m in mates:
        copies.append(send(slots.at[m], arrived.at[e], sends, receives, len(copies), {"expert": m}))
    mine = rows.at[:, pl.ds(pl.multiple_of(g * width, width), width)]
    local_copies = [
        pltpu.make_async_copy(dest, dest_all.at[g], own.at[0]),
        pltpu.make_async_copy(mine, columns.at[g], own.at[1]),
        pltpu.make_async_copy(slots.at[e], arrived.at[e], own.at[2]),
    ]
    for copy in local_copies:
        copy.start()
    for copy in copies:
        copy.wait()
    for copy in local_copies:
        copy.wait()


def first_exchange(rows, dest, slots, groups, experts):
    row_count, model_width = rows.shape
    count = 2 * (groups - 1) + experts - 1
    anywhere = pl.BlockSpec(memory_space=pl.ANY)
    return pl.pallas_call(
        functools.partial(first_kernel, groups, experts),
        out_shape=(
            jax.ShapeDtypeStruct((groups, row_count, model_width // groups), rows.dtype),
            jax.ShapeDtypeStruct((groups,) + dest.shape, dest.dtype),
            jax.ShapeDtypeStruct(slots.shape, slots.dtype),
        ),
        in_specs=[anywhere] * 3,
        out_specs=(anywhere,) * 3,
        scratch_shapes=[
            pltpu.SemaphoreType.DMA((count,)),
            pltpu.SemaphoreType.DMA((count,)),
            pltpu.SemaphoreType.DMA((3,)),
        ],
        compiler_params=pltpu.CompilerParams(collective_id=1, has_side_effects=True),
        name="first_exchange",
    )(rows, dest, slots)


def second_kernel(experts, slots, arrived, sends, receives, own):
    e = lax.axis_index("expert")
    mates = [lax.rem(e + k, experts) for k in range(1, experts)]
    greet([{"expert": m} for m in mates])
    copies = []
    for m in mates:
        copies.append(
            send(slots.at[:, m], arrived.at[:, e], sends, receives, len(copies), {"expert": m})
        )
    local_copy = pltpu.make_async_copy(slots.at[:, e], arrived.at[:, e], own)
    local_copy.start()
    for copy in copies:
        copy.wait()
    local_copy.wait()


def expert_exchange(slots, experts, number, weight=32):
    anywhere = pl.BlockSpec(memory_space=pl.ANY)
    return pl.pallas_call(
        functools.partial(second_kernel, experts),
        out_shape=jax.ShapeDtypeStruct(slots.shape, slots.dtype),
        in_specs=[anywhere],
        out_specs=anywhere,
        scratch_shapes=[
            pltpu.SemaphoreType.DMA((experts - 1,)),
            pltpu.SemaphoreType.DMA((experts - 1,)),
            pltpu.SemaphoreType.DMA,
        ],
        cost_estimate=pl.CostEstimate(
            flops=0, bytes_accessed=weight * slots.size * slots.dtype.itemsize, transcendentals=0
        ),
        compiler_params=pltpu.CompilerParams(collective_id=number, has_side_effects=True),
    )(slots)


def local(out_grad, destination, hidden, weight, left_prev, right_prev):
    expert_count = lax.axis_size("expert")
    group_count = lax.axis_size("dp")
    row_count, model_width = out_grad.shape
    slot_count, hidden_width = hidden.shape
    capacity = slot_count // expert_count
    half_width = model_width // group_count
    block_width = 2 * half_width

    hidden_all = lax.all_gather(hidden, "dp", axis=0, tiled=True)
    target_slots, own_choice = slot_choice(destination[:, 0], expert_count, capacity)
    outgoing = jnp.dot(own_choice, out_grad, preferred_element_type=jnp.float32).astype(
        out_grad.dtype
    )
    column_rows, dest_all, arrived = first_exchange(
        out_grad,
        destination.reshape(row_count // 128, 128),
        outgoing.reshape(expert_count, capacity, model_width),
        group_count,
        expert_count,
    )
    arrived = arrived.reshape(slot_count, model_width)
    group = lax.axis_index("dp")
    helped = group_count == 4
    if helped:
        inward, across, outward = [(0, 1), (3, 2)], [(1, 2), (2, 1)], [(1, 0), (2, 3)]
        weight_in = lax.ppermute(weight[0], "dp", inward)
        weight_late, weight_mid, rows_late, column_rows = lax.optimization_barrier(
            (weight[0], weight_in, out_grad, column_rows)
        )
        weight_across = lax.ppermute(weight_late, "dp", across)
        weight_far = lax.ppermute(weight_mid, "dp", across)
        rows_in = lax.ppermute(rows_late, "dp", inward)
    else:
        weight_late, column_rows = lax.optimization_barrier((weight[0], column_rows))
        weight_all = lax.all_gather(weight_late, "dp", axis=0)

    _, all_choice = slot_choice(dest_all.reshape(group_count, row_count), expert_count, capacity)
    column_slots = lax.dot_general(
        all_choice,
        column_rows,
        (((2,), (1,)), ((0,), (0,))),
        preferred_element_type=jnp.float32,
    ).astype(out_grad.dtype)
    columns = expert_exchange(
        column_slots.reshape(group_count, expert_count, capacity, half_width),
        expert_count,
        2,
        1,
    )
    hidden_slots = hidden_all
    own_piece = lax.dot_general(
        columns.reshape(-1, half_width),
        hidden_slots,
        (((0,), (0,)), ((), ())),
        preferred_element_type=jnp.float32,
    ).astype(jnp.bfloat16)
    partner = swapped(own_piece, "dp", 0)
    parity = lax.axis_index("dp") % 2
    upper_half = parity == 0
    first_half = jnp.where(upper_half, own_piece, partner)
    second_half = jnp.where(upper_half, partner, own_piece)
    block_grad = jnp.concatenate([first_half, second_half], axis=0)
    scale_left = 1.0 / (group_count * row_count * block_width)
    scale_right = 1.0 / (group_count * row_count * hidden_width)
    right_gram = (
        lax.dot_general(
            own_piece,
            block_grad,
            (((1,), (1,)), ((), ())),
            preferred_element_type=jnp.float32,
        )
        * scale_right
    )
    half_hidden = hidden_width // 2
    hidden_cols = lax.dynamic_slice_in_dim(block_grad, parity * half_hidden, half_hidden, 1)
    left_gram = (
        lax.dot_general(
            hidden_cols,
            block_grad,
            (((0,), (0,)), ((), ())),
            preferred_element_type=jnp.float32,
        )
        * scale_left
    )
    left_stats = ema_decay * left_prev + (1.0 - ema_decay) * left_gram[None]
    right_stats = ema_decay * right_prev + (1.0 - ema_decay) * right_gram[None]

    def against(values, part, weight_part):
        taken = lax.dynamic_slice_in_dim(values, part * half_width, half_width, 1)
        return lax.dot_general(
            taken, weight_part, (((1,), (1,)), ((), ())), preferred_element_type=jnp.float32
        )

    if helped:
        pair = group ^ 1
        arrived, rows_in, _ = lax.optimization_barrier((arrived, rows_in, own_piece))
        pair_dest = lax.dynamic_index_in_dim(dest_all, pair, 0, keepdims=False)
        pair_slots, pair_choice = slot_choice(
            pair_dest.reshape(row_count), expert_count, capacity
        )
        pair_outgoing = jnp.dot(
            pair_choice, rows_in, preferred_element_type=jnp.float32
        ).astype(out_grad.dtype)
        pair_arrived = expert_exchange(
            pair_outgoing.reshape(1, expert_count, capacity, model_width), expert_count, 3
        ).reshape(slot_count, model_width)
        far = group_count - 1 - group
        weight_across, weight_far, pair_arrived, _ = lax.optimization_barrier(
            (weight_across, weight_far, pair_arrived, partner)
        )
        held = (
            (group, weight_late),
            (pair, weight_in),
            (far, weight_across),
            (far ^ 1, weight_far),
        )
        slot_grads = jnp.stack(
            [
                sum(against(values, part, piece) for part, piece in held).astype(jnp.bfloat16)
                for values in (arrived, pair_arrived)
            ]
        )
        returned = expert_exchange(
            slot_grads.reshape(2, expert_count, capacity, hidden_width), expert_count, 4
        ).reshape(2, slot_count, hidden_width)
        own_rows = returned[0][target_slots]
        pair_rows = lax.ppermute(returned[1][pair_slots], "dp", outward)
        own_rows, _, _ = lax.optimization_barrier((own_rows, left_stats, right_stats))
        inner = (group == 1) | (group == 2)
        grad_rows = jnp.where(inner, own_rows, pair_rows)
        return (grad_rows, left_stats, right_stats)

    arrived, _, _ = lax.optimization_barrier((arrived, left_stats, right_stats))
    slot_grad = sum(against(arrived, part, weight_all[part]) for part in range(group_count)).astype(
        jnp.bfloat16
    )
    returned = expert_exchange(
        slot_grad.reshape(1, expert_count, capacity, hidden_width), expert_count, 4
    )
    grad_rows = returned.reshape(slot_count, hidden_width)[target_slots]
    return (grad_rows, left_stats, right_stats)


def solution(mesh):
    placed = (
        P(("dp", "expert"), None),
        P(("dp", "expert"), None),
        P(("dp", "expert"), None),
        P("expert", None, "dp"),
        P("expert", "dp", None),
        P("expert", "dp", None),
    )

    return jax.shard_map(
        local,
        mesh=mesh,
        in_specs=placed,
        out_specs=(P(("dp", "expert"), None), P("expert", "dp", None), P("expert", "dp", None)),
        check_vma=False,
    )
```
